32 devices in a mesh: dp: 8 (over y, x, core), tensor: 4 (over z).
Axes of the slice: x: 2, y: 2, z: 4, core: 2. Of those that a mesh axis runs over, the one named last changes fastest.
Arguments:
- inputs: bfloat16 [768, 32768], P('tensor', 'dp'), may hold values from -18 to 18
- cotangent: float32 [768, 32768], P('tensor', 'dp'), may hold values from -18 to 18
- query_w: bfloat16 [768, 192], P('tensor'), may hold values from -0.21875 to 0.21875
- key_w: bfloat16 [768, 192], P('tensor'), may hold values from -0.21875 to 0.21875
- value_w: bfloat16 [768, 192], P('tensor'), may hold values from -0.4375 to 0.4375
- query_b: float32 [768], P('tensor'), may hold values from -1.75 to 1.75
- value_b: float32 [768], P('tensor'), may hold values from -0.0625 to 0.0625
- output_w: bfloat16 [768, 768], P(None, 'tensor'), may hold values from -4 to 4
- output_b: float32 [768], P('tensor'), may hold values from -1.25 to 1.25
- first_gain: float32 [768], P('tensor'), may hold values from 0.5 to 1.5
- first_shift: float32 [768], P('tensor'), may hold values from -1.25 to 1.25
- inner_w: bfloat16 [3072, 192], P('tensor'), may hold values from -0.4375 to 0.4375
- inner_b: float32 [3072], P('tensor'), may hold values from -1.25 to 1.25
- outer_w: bfloat16 [768, 768], P('tensor'), may hold values from -0.21875 to 0.21875
- outer_b: float32 [768], P('tensor'), may hold values from -1.25 to 1.25
- second_gain: float32 [768], P('tensor'), may hold values from 0.5 to 1.5
- second_shift: float32 [768], P('tensor'), may hold values from -1.25 to 1.25
Outputs:
- layer_out: bfloat16 [768, 32768], P('tensor', 'dp')
- input_grad: bfloat16 [768, 32768], P('tensor', 'dp')
- grad_query_w: float32 [768, 192], P('tensor')
- grad_key_w: float32 [768, 192], P('tensor')
- grad_value_w: float32 [768, 192], P('tensor')
- grad_query_b: float32 [768], P('tensor')
- grad_value_b: float32 [768], P('tensor')
- grad_output_w: float32 [768, 768], P(None, 'tensor')
- grad_output_b: float32 [768], P('tensor')
- grad_first_gain: float32 [768], P('tensor')
- grad_first_shift: float32 [768], P('tensor')
- grad_inner_w: float32 [3072, 192], P('tensor')
- grad_inner_b: float32 [3072], P('tensor')
- grad_outer_w: float32 [768, 768], P('tensor')
- grad_outer_b: float32 [768], P('tensor')
- grad_second_gain: float32 [768], P('tensor')
- grad_second_shift: float32 [768], P('tensor')
The draws below stay inside these ranges and needn't reach their ends.
All inputs are finite; a program needn't handle non-finite values.
Results may differ from the reference program's by a relative error of at most 0.0095.
Values may be sent and summed in bfloat16 or wider, within the bound.
No kernel may reach another device: no remote copies, remote signals or barrier semaphores. Data moves between devices by JAX's collectives and lax.ppermute only.
A program may use at most 128 MiB of HBM per device.

```python
import jax
import jax.numpy as jnp
from jax import lax

D = 768
HEADS = 12
HDIM = 64
FF = 3072
GROUPS = 4
SEQ_LEN = 1024
TOKENS = 32768


def draw_inputs(key, part):
    noise = jax.random.normal(key, (D, TOKENS), jnp.float32)
    rising = 1.0 + 2.0 * jnp.arange(D, dtype=jnp.float32)[:, None] / D
    return (jnp.clip(noise, -6.0, 6.0) * rising).astype(jnp.bfloat16)


def draw_cotangent(key, part):
    noise = jax.random.normal(key, (D, TOKENS), jnp.float32)
    rising = 1.0 + 2.0 * jnp.arange(TOKENS, dtype=jnp.float32)[None, :] / TOKENS
    return jnp.clip(noise, -6.0, 6.0) * rising


def block_levels(rng, shape, shards, least, high):
    factor_of, own = 1.0, jax.random.fold_in(rng, 6)
    for dim, parts in shards:
        draws = jnp.exp(jax.random.uniform(jax.random.fold_in(own, dim), (parts,), jnp.float32, least / len(shards), high / len(shards)))
        factor_of = factor_of * jnp.repeat(draws, shape[dim] // parts).reshape([-1 if axis == dim else 1 for axis in range(len(shape))])
    return factor_of


def bell_draw(own_key, extent, scale, reach, shards=(), held_as=jnp.bfloat16):
    values = scale * jax.random.normal(own_key, extent, jnp.float32)
    if shards:
        values = values * block_levels(own_key, extent, shards, -0.22, 0.18)
    return jnp.clip(values, -reach, reach).astype(held_as)


def setup_inputs(seed: int = 0) -> dict:
    arg_keys = jax.random.split(jax.random.key(seed), 18)
    inputs = draw_inputs(jax.random.fold_in(arg_keys[17], 71), 0)
    cotangent = draw_cotangent(jax.random.fold_in(arg_keys[17], 71), 0)
    query_w = bell_draw(arg_keys[2], (D, D // GROUPS), (4 * (D // GROUPS)) ** -0.5, 0.21875, ((0, 4),))
    key_w = bell_draw(arg_keys[3], (D, D // GROUPS), (4 * (D // GROUPS)) ** -0.5, 0.21875, ((0, 4),))
    value_w = bell_draw(arg_keys[4], (D, D // GROUPS), (D // GROUPS) ** -0.5, 0.4375, ((0, 4),))
    query_b = bell_draw(arg_keys[5], (D,), 0.3, 1.75, ((0, 4),), jnp.float32)
    value_b = bell_draw(arg_keys[6], (D,), 0.01, 0.0625, ((0, 4),), jnp.float32)
    output_w = bell_draw(arg_keys[7], (D, D), 2 ** -0.5, 4.0, ((1, 4),))
    output_b = bell_draw(arg_keys[8], (D,), 0.2, 1.25, ((0, 4),), jnp.float32)
    first_gain = jnp.clip(1.0 + 0.1 * jax.random.normal(arg_keys[9], (D,), jnp.float32), 0.5, 1.5)
    first_shift = bell_draw(arg_keys[10], (D,), 0.2, 1.25, ((0, 4),), jnp.float32)
    inner_w = bell_draw(arg_keys[11], (FF, D // GROUPS), (D // GROUPS) ** -0.5, 0.4375, ((0, 4),))
    inner_b = bell_draw(arg_keys[12], (FF,), 0.2, 1.25, ((0, 4),), jnp.float32)
    outer_w = bell_draw(arg_keys[13], (D, FF // GROUPS), (FF // GROUPS) ** -0.5, 0.21875, ((0, 4),))
    outer_b = bell_draw(arg_keys[14], (D,), 0.2, 1.25, ((0, 4),), jnp.float32)
    second_gain = jnp.clip(1.0 + 0.1 * jax.random.normal(arg_keys[15], (D,), jnp.float32), 0.5, 1.5)
    second_shift = bell_draw(arg_keys[16], (D,), 0.2, 1.25, ((0, 4),), jnp.float32)
    return {"inputs": inputs, "cotangent": cotangent, "query_w": query_w, "key_w": key_w, "value_w": value_w, "query_b": query_b, "value_b": value_b, "output_w": output_w, "output_b": output_b, "first_gain": first_gain, "first_shift": first_shift, "inner_w": inner_w, "inner_b": inner_b, "outer_w": outer_w, "outer_b": outer_b, "second_gain": second_gain, "second_shift": second_shift}


HIGH = lax.Precision.HIGHEST
EPSILON = 1e-05

@jax.custom_vjp
def low(v):
    return lax.optimization_barrier(v.astype(jnp.bfloat16)).astype(jnp.float32)

@jax.custom_vjp
def low_back(v):
    return v

def low_keep(v):
    return (low(v), None)

def low_pass(kept, grad):
    return (grad,)

def back_keep(v):
    return (v, None)

def back_low(kept, grad):
    return (low(grad),)
low.defvjp(low_keep, low_pass)
low_back.defvjp(back_keep, back_low)

def grouped(weight, operand):
    rows = weight.shape[0] // GROUPS
    blocks = weight.reshape(GROUPS, rows, weight.shape[1])
    pieces = operand.reshape(GROUPS, weight.shape[1], operand.shape[1])
    return jnp.einsum('goi,gil->gol', blocks, pieces, precision=HIGH).reshape(GROUPS * rows, operand.shape[1])

def normalize(resid, gain, shift):
    center = lax.optimization_barrier(jnp.mean(resid, axis=0, keepdims=True))
    offset = resid - center
    spread = lax.optimization_barrier(jnp.mean(offset * offset, axis=0, keepdims=True))
    return offset * lax.rsqrt(spread + EPSILON) * gain[:, None] + shift[:, None]

def layer(params, sequence):
    query_w, key_w, value_w, query_b, value_b, output_w, output_b, first_gain, first_shift, inner_w, inner_b, outer_w, outer_b, second_gain, second_shift = params
    length = sequence.shape[1]
    query = low(low_back(grouped(query_w, sequence) + query_b[:, None]))
    keys = low(low_back(grouped(key_w, sequence)))
    values = low(low_back(grouped(value_w, sequence) + value_b[:, None]))
    query_heads = query.reshape(HEADS, HDIM, length)
    key_heads = keys.reshape(HEADS, HDIM, length)
    value_heads = values.reshape(HEADS, HDIM, length)
    scores = low_back(jnp.einsum('hdq,hdk->hqk', query_heads, key_heads, precision=HIGH) * HDIM ** (-0.5))
    probs = low(jax.nn.softmax(scores, axis=-1))
    context = jnp.einsum('hqk,hdk->hdq', probs, value_heads, precision=HIGH).reshape(D, length)
    context = low(low_back(context))
    attended = low_back(jnp.dot(output_w, context, precision=HIGH) + output_b[:, None])
    first_hidden = normalize(sequence + attended, first_gain, first_shift)
    inner = low_back(grouped(inner_w, low(first_hidden)) + inner_b[:, None])
    activ = low(jax.nn.gelu(inner, approximate=False))
    outer = low_back(grouped(outer_w, activ) + outer_b[:, None])
    return normalize(first_hidden + outer, second_gain, second_shift)

def reference(inputs, cotangent, query_w, key_w, value_w, query_b, value_b, output_w, output_b, first_gain, first_shift, inner_w, inner_b, outer_w, outer_b, second_gain, second_shift):
    params = tuple((p.astype(jnp.float32) for p in (query_w, key_w, value_w, query_b, value_b, output_w, output_b, first_gain, first_shift, inner_w, inner_b, outer_w, outer_b, second_gain, second_shift)))
    number = TOKENS // SEQ_LEN
    seq_inputs = jnp.transpose(inputs.astype(jnp.float32).reshape(D, number, SEQ_LEN), (1, 0, 2))
    seq_cots = jnp.transpose(cotangent.astype(jnp.float32).reshape(D, number, SEQ_LEN), (1, 0, 2))
    zeros = tuple((jnp.zeros_like(p) for p in params))

    def one_sequence(total, pair):
        sequence, seq_cot = pair
        result, pull_back = jax.vjp(layer, params, sequence)
        grad_params, grad_sequence = pull_back(seq_cot)
        total = tuple((a + b for a, b in zip(total, grad_params)))
        return (total, (result.astype(jnp.bfloat16), grad_sequence.astype(jnp.bfloat16)))
    total, (results, grads) = lax.scan(one_sequence, zeros, (seq_inputs, seq_cots))
    layer_out = jnp.transpose(results, (1, 0, 2)).reshape(D, TOKENS)
    input_grad = jnp.transpose(grads, (1, 0, 2)).reshape(D, TOKENS)
    return (layer_out, input_grad, total[0], total[1], total[2], total[3], total[4], total[5], total[6], total[7], total[8], total[9], total[10], total[11], total[12], total[13], total[14])
```

```python
from functools import partial

import jax
import jax.numpy as jnp
from jax import lax
from jax.experimental import pallas as pl
from jax.experimental.pallas import tpu as pltpu
from jax.sharding import PartitionSpec as P

D = 768
HDIM = 64
SEQ_LEN = 1024
EPSILON = 1e-05
SCALE = HDIM ** (-0.5)
CHUNK = 256
TOKEN_BLOCK = 256

F32 = jnp.float32
BF16 = jnp.bfloat16


def mm(left, right):
    return lax.dot_general(left, right, (((1,), (0,)), ((), ())), preferred_element_type=F32)


def mm_nt(left, right):
    return lax.dot_general(left, right, (((1,), (1,)), ((), ())), preferred_element_type=F32)


def mm_tn(left, right):
    return lax.dot_general(left, right, (((0,), (0,)), ((), ())), preferred_element_type=F32)


def attend_kernel(x_ref, w_ref, b_ref, qkv_ref, ctx_ref, expo_ref, inv_ref):
    rows = 3 * HDIM
    weight = w_ref[...].reshape(rows, w_ref.shape[2])
    bias = b_ref[...].reshape(rows, 1)
    low = (mm(weight, x_ref[...]) + bias).astype(BF16)
    qkv_ref[...] = low.reshape(3, HDIM, low.shape[1])
    query = low[:HDIM] * BF16(SCALE)
    keys = low[HDIM : 2 * HDIM]
    values = low[2 * HDIM :]
    for start in range(0, low.shape[1], CHUNK):
        part = slice(start, start + CHUNK)
        scores = mm_tn(keys, query[:, part])
        expo = jnp.exp(scores - jnp.max(scores, axis=0, keepdims=True))
        inv = 1.0 / jnp.sum(expo, axis=0, keepdims=True)
        expo_low = expo.astype(BF16)
        expo_ref[0, :, part] = expo_low
        inv_ref[0, :, part] = inv
        ctx_ref[:, part] = (mm(values, expo_low) * inv).astype(BF16)


def attend(x, weight, bias):
    local, length = x.shape
    heads = local // HDIM
    return pl.pallas_call(
        attend_kernel,
        grid=(heads,),
        in_specs=[
            pl.BlockSpec((local, length), lambda h: (0, 0)),
            pl.BlockSpec((3, HDIM, local), lambda h: (0, h, 0)),
            pl.BlockSpec((3, HDIM, 1), lambda h: (0, h, 0)),
        ],
        out_specs=[
            pl.BlockSpec((3, HDIM, length), lambda h: (0, h, 0)),
            pl.BlockSpec((HDIM, length), lambda h: (h, 0)),
            pl.BlockSpec((1, length, length), lambda h: (h, 0, 0)),
            pl.BlockSpec((1, 1, length), lambda h: (h, 0, 0)),
        ],
        out_shape=[
            jax.ShapeDtypeStruct((3, local, length), BF16),
            jax.ShapeDtypeStruct((local, length), BF16),
            jax.ShapeDtypeStruct((heads, length, length), BF16),
            jax.ShapeDtypeStruct((heads, 1, length), F32),
        ],
        name="attend",
    )(x, weight, bias)


def attend_back_kernel(
    x_ref, w_ref, qkv_ref, ctx_ref, expo_ref, inv_ref, grad_ref, resid_ref, out_ref, gw_ref, gb_ref, acc_ref
):
    head = pl.program_id(0)
    rows = 3 * HDIM
    length = x_ref.shape[1]
    query = qkv_ref[0]
    keys = qkv_ref[1]
    values = qkv_ref[2]
    scaled = (grad_ref[...].astype(F32) * inv_ref[0]).astype(BF16)
    delta = jnp.sum(scaled.astype(F32) * ctx_ref[...].astype(F32), axis=0, keepdims=True)
    grad_keys = jnp.zeros((HDIM, length), F32)
    grad_values = jnp.zeros((HDIM, length), F32)
    grad_query = []
    for start in range(0, length, CHUNK):
        part = slice(start, start + CHUNK)
        expo = expo_ref[0, :, part]
        grad_probs = mm_tn(values, scaled[:, part])
        grad_scores = (expo.astype(F32) * (grad_probs - delta[:, part])).astype(BF16)
        grad_query.append((mm(keys, grad_scores) * SCALE).astype(BF16))
        grad_keys += mm_nt(query[:, part], grad_scores)
        grad_values += mm_nt(scaled[:, part], expo)
    low = jnp.concatenate(
        [
            jnp.concatenate(grad_query, axis=1),
            (grad_keys * SCALE).astype(BF16),
            grad_values.astype(BF16),
        ],
        axis=0,
    )
    gw_ref[...] = mm_nt(low, x_ref[...]).reshape(3, HDIM, x_ref.shape[0])
    gb_ref[...] = jnp.sum(low.astype(F32), axis=1, keepdims=True).reshape(3, HDIM, 1)
    step = mm_tn(w_ref[...].reshape(rows, x_ref.shape[0]), low)

    @pl.when(head == 0)
    def _():
        acc_ref[...] = resid_ref[...] + step

    @pl.when(head > 0)
    def _():
        acc_ref[...] += step

    @pl.when(head == pl.num_programs(0) - 1)
    def _():
        out_ref[...] = acc_ref[...].astype(BF16)


def attend_back(x, weight, qkv, context, expo, inv, grad_context, grad_resid):
    local, length = x.shape
    heads = local // HDIM
    return pl.pallas_call(
        attend_back_kernel,
        grid=(heads,),
        in_specs=[
            pl.BlockSpec((local, length), lambda h: (0, 0)),
            pl.BlockSpec((3, HDIM, local), lambda h: (0, h, 0)),
            pl.BlockSpec((3, HDIM, length), lambda h: (0, h, 0)),
            pl.BlockSpec((HDIM, length), lambda h: (h, 0)),
            pl.BlockSpec((1, length, length), lambda h: (h, 0, 0)),
            pl.BlockSpec((1, 1, length), lambda h: (h, 0, 0)),
            pl.BlockSpec((HDIM, length), lambda h: (h, 0)),
            pl.BlockSpec((local, length), lambda h: (0, 0)),
        ],
        out_specs=[
            pl.BlockSpec((local, length), lambda h: (0, 0)),
            pl.BlockSpec((3, HDIM, local), lambda h: (0, h, 0)),
            pl.BlockSpec((3, HDIM, 1), lambda h: (0, h, 0)),
        ],
        out_shape=[
            jax.ShapeDtypeStruct((local, length), BF16),
            jax.ShapeDtypeStruct((3, local, local), F32),
            jax.ShapeDtypeStruct((3, local, 1), F32),
        ],
        scratch_shapes=[pltpu.VMEM((local, length), F32)],
        name="attend_back",
    )(x, weight, qkv, context, expo, inv, grad_context, grad_resid)


def normal_parts(v):
    expo = jnp.exp(-0.5 * v * v)
    t = 1.0 / (1.0 + (0.3275911 * 0.5**0.5) * jnp.abs(v))
    poly = t * (
        0.127414796 + t * (-0.142248368 + t * (0.7107068705 + t * (-0.7265760135 + t * 0.5307027145)))
    )
    tail = poly * expo
    return jnp.where(v >= 0, 1.0 - tail, tail), expo * 0.3989422804014327


V_OUT_B, V_GAIN1, V_SHIFT1, V_OUTER_B, V_GAIN2, V_SHIFT2, V_INNER_B = range(7)
G_OUT_B, G_GAIN1, G_SHIFT1, G_OUTER_B, G_GAIN2, G_INNER_B = range(6)


def middle_kernel(
    groups,
    rank_ref,
    *refs,
):
    x_refs = refs[:groups]
    ctx_refs = refs[groups : 2 * groups]
    cot_refs = refs[2 * groups : 3 * groups]
    w_ref, vec_ref = refs[3 * groups : 3 * groups + 2]
    refs = refs[3 * groups + 2 :]
    out_refs = refs[:groups]
    grad_refs = refs[groups : 2 * groups]
    resid_refs = refs[2 * groups : 3 * groups]
    gw_ref, gv_ref, act_ref, dact_ref = refs[3 * groups :]
    span = range(groups)
    local = x_refs[0].shape[0]
    hidden = w_ref.shape[2]
    first = pl.program_id(0) == 0
    rank = rank_ref[0]
    rows = [pl.ds(pl.multiple_of(lax.rem(rank + r, groups) * local, local), local) for r in span]

    @pl.when(first)
    def _():
        gw_ref[...] = jnp.zeros_like(gw_ref)
        gv_ref[...] = jnp.zeros_like(gv_ref)

    def vec(r, which):
        return vec_ref[r, :, which : which + 1]

    def total(parts):
        return sum(jnp.sum(p, axis=0, keepdims=True) for p in parts)

    def add_vec(r, which, array):
        gv_ref[r, :, which : which + 1] += jnp.sum(array, axis=1, keepdims=True)

    ctx = [ctx_refs[r][...] for r in span]
    resid = []
    for o in span:
        attended = sum(mm(w_ref[r, 0, rows[o], :], ctx[r]) for r in span)
        resid.append(x_refs[o][...].astype(F32) + attended + vec(o, V_OUT_B))
    center = total(resid) / D
    offset = [p - center for p in resid]
    inv1 = lax.rsqrt(total([p * p for p in offset]) / D + EPSILON)
    normed1 = [p * inv1 for p in offset]
    low1 = []
    resid2 = []
    for r in span:
        hid = normed1[r] * vec(r, V_GAIN1) + vec(r, V_SHIFT1)
        low = hid.astype(BF16)
        low1.append(low)
        inner = mm(w_ref[r, 1], low)
        outer = hid + vec(r, V_OUTER_B)
        for part in range(hidden // local):
            at = slice(part * local, (part + 1) * local)
            v = inner[at] + vec(r, V_INNER_B + part)
            cdf, density = normal_parts(v)
            act = (v * cdf).astype(BF16)
            act_ref[r, at, :] = act
            dact_ref[r, at, :] = cdf + v * density
        outer += mm_tn(w_ref[r, 2], act_ref[r])
        resid2.append(outer)
    center = total(resid2) / D
    offset = [p - center for p in resid2]
    inv2 = lax.rsqrt(total([p * p for p in offset]) / D + EPSILON)
    normed2 = [p * inv2 for p in offset]
    scaled = []
    for r in span:
        out_refs[r][...] = (normed2[r] * vec(r, V_GAIN2) + vec(r, V_SHIFT2)).astype(BF16)
        cot = cot_refs[r][...].astype(F32)
        add_vec(r, G_GAIN2, cot * normed2[r])
        scaled.append(cot * vec(r, V_GAIN2))
    mean = total(scaled) / D
    slope = total([scaled[r] * normed2[r] for r in span]) / D
    grad1 = []
    for r in span:
        grad2 = inv2 * (scaled[r] - mean - normed2[r] * slope)
        grad2_low = grad2.astype(BF16)
        add_vec(r, G_OUTER_B, grad2_low.astype(F32))
        gw_ref[r, 2] += mm_nt(act_ref[r], grad2_low)
        grad_act = mm(w_ref[r, 2], grad2_low)
        pieces = []
        for part in range(hidden // local):
            at = slice(part * local, (part + 1) * local)
            piece = (grad_act[at] * dact_ref[r, at, :]).astype(BF16)
            add_vec(r, G_INNER_B + part, piece.astype(F32))
            pieces.append(piece)
        inner_low = jnp.concatenate(pieces, axis=0)
        gw_ref[r, 1] += mm_nt(inner_low, low1[r])
        grad = grad2 + mm_tn(w_ref[r, 1], inner_low)
        add_vec(r, G_GAIN1, grad * normed1[r])
        add_vec(r, G_SHIFT1, grad)
        grad1.append(grad)
    scaled = [grad1[r] * vec(r, V_GAIN1) for r in span]
    mean = total(scaled) / D
    slope = total([scaled[r] * normed1[r] for r in span]) / D
    lows = []
    for r in span:
        grad = inv1 * (scaled[r] - mean - normed1[r] * slope)
        resid_refs[r][...] = grad
        low = grad.astype(BF16)
        lows.append(low)
        add_vec(r, G_OUT_B, low.astype(F32))
    for r in span:
        context_grad = sum(mm_tn(w_ref[r, 0, rows[o], :], lows[o]) for o in span)
        grad_refs[r][...] = context_grad.astype(BF16)
        for o in span:
            gw_ref[r, 0, rows[o], :] += mm_nt(lows[o], ctx[r])


def middle(rank, xs, contexts, cots, weights, vecs):
    groups = len(xs)
    local, length = xs[0].shape
    hidden = weights.shape[2]
    block = pl.BlockSpec((local, TOKEN_BLOCK), lambda t, rank: (0, t))
    whole = lambda shape: pl.BlockSpec(
        shape, lambda t, rank: (0,) * len(shape), pipeline_mode=pl.Buffered(1)
    )
    grad_vecs = (groups, local, G_INNER_B + hidden // local)
    piece = lambda dtype: jax.ShapeDtypeStruct((local, length), dtype)
    outs = pl.pallas_call(
        partial(middle_kernel, groups),
        grid_spec=pltpu.PrefetchScalarGridSpec(
            num_scalar_prefetch=1,
            grid=(length // TOKEN_BLOCK,),
            in_specs=[block] * (3 * groups) + [whole(weights.shape), whole(vecs.shape)],
            out_specs=[block] * (3 * groups) + [whole(weights.shape), whole(grad_vecs)],
            scratch_shapes=[
                pltpu.VMEM((groups, hidden, TOKEN_BLOCK), BF16),
                pltpu.VMEM((groups, hidden, TOKEN_BLOCK), F32),
            ],
        ),
        out_shape=[piece(BF16)] * (2 * groups)
        + [piece(F32)] * groups
        + [
            jax.ShapeDtypeStruct(weights.shape, F32),
            jax.ShapeDtypeStruct(grad_vecs, F32),
        ],
        name="middle",
    )(rank, *xs, *contexts, *cots, weights, vecs)
    return (
        outs[:groups],
        outs[groups : 2 * groups],
        outs[2 * groups : 3 * groups],
        outs[3 * groups],
        outs[3 * groups + 1],
    )


def shards(
    inputs,
    cotangent,
    query_w,
    key_w,
    value_w,
    query_b,
    value_b,
    output_w,
    output_b,
    first_gain,
    first_shift,
    inner_w,
    inner_b,
    outer_w,
    outer_b,
    second_gain,
    second_shift,
):
    groups = lax.axis_size("tensor")
    rank = lax.axis_index("tensor")
    number = lax.axis_size("dp")
    place = lax.axis_index("dp")
    local, tokens = inputs.shape
    length = tokens // groups
    span = range(groups)
    assert length == SEQ_LEN

    def from_group(piece, r):
        if r == 0:
            return piece
        return lax.ppermute(piece, "tensor", [(i, (i - r) % groups) for i in span])

    def to_group(piece, r):
        if r == 0:
            return piece
        return lax.ppermute(piece, "tensor", [(i, (i + r) % groups) for i in span])

    def swap(piece, bit):
        return lax.ppermute(piece, "dp", [(i, i ^ bit) for i in range(number)])

    def part_for(array, r):
        owner = lax.rem(rank + groups - r, groups)
        return lax.dynamic_slice_in_dim(array, owner * length, length, 1)

    def assemble(pieces):
        whole = jnp.zeros((local, tokens), pieces[0].dtype)
        for r in span:
            owner = lax.rem(rank + groups - r, groups)
            whole = lax.dynamic_update_slice_in_dim(whole, to_group(pieces[r], r), owner * length, 1)
        return whole

    def half(array, bit, other):
        size = array.shape[1] // 2
        which = lax.rem(lax.div(place, bit), 2)
        which = 1 - which if other else which
        return lax.dynamic_slice_in_dim(array, which * size, size, 1)

    def join(mine, got, bit, axis):
        first = lax.rem(lax.div(place, bit), 2) == 0
        return jnp.where(
            first,
            jnp.concatenate([mine, got], axis=axis),
            jnp.concatenate([got, mine], axis=axis),
        )

    bits = [1 << k for k in range(number.bit_length() - 1)]
    mirrored = sum(lax.rem(lax.div(place, bit), 2) * (number // 2 // bit) for bit in bits)

    def all_groups(shard, axis):
        size = shard.shape[axis] // number
        mine = lax.dynamic_slice_in_dim(shard, mirrored * size, size, axis)
        held = jnp.stack([from_group(mine, r) for r in span[1:]])
        for bit in reversed(bits):
            held = join(held, swap(held, bit), bit, axis + 1)
        return [shard] + [held[r - 1] for r in span[1:]]

    def reduce_groups(parts):
        for bit in bits:
            got = swap(half(parts, bit, True).astype(BF16), bit)
            parts = half(parts, bit, False) + got.astype(F32)
        total = parts[0]
        for r in span[1:]:
            total = total + to_group(parts[r].astype(BF16), r).astype(F32)
        for bit in reversed(bits):
            total = join(total, swap(total, bit), bit, 0)
        return total

    xs = [from_group(part_for(inputs, r), r) for r in span]
    vec_shard = jnp.concatenate(
        [
            jnp.stack(
                [
                    output_b,
                    first_gain,
                    first_shift,
                    outer_b,
                    second_gain,
                    second_shift,
                ]
            ),
            inner_b.reshape(-1, local),
            jnp.stack([query_b, jnp.zeros_like(query_b), value_b]),
        ]
    )
    vec_rows = [from_group(vec_shard, r) for r in span]
    qkv_w = all_groups(jnp.stack([query_w, key_w, value_w]), 1)
    mid_w = all_groups(jnp.stack([output_w, inner_w, outer_w.T]), 1)
    cot_low = cotangent.astype(BF16)
    cots = [from_group(part_for(cot_low, r), r) for r in span]

    saved = []
    for r in span:
        bias = vec_rows[r][-3:][:, :, None]
        saved.append(attend(xs[r], qkv_w[r], bias))
    vecs = jnp.swapaxes(jnp.stack([rows[:-3] for rows in vec_rows]), 1, 2)
    outs, grad_contexts, grad_resids, grad_mid_w, grad_vecs = middle(
        rank.reshape(1), xs, [s[1] for s in saved], cots, jnp.stack(mid_w), vecs
    )
    layer_out = assemble(outs)
    backs = [None] * groups
    for r in (2, 3, 1, 0):
        qkv, context, expo, inv = saved[r]
        backs[r] = attend_back(
            xs[r], qkv_w[r], qkv, context, expo, inv, grad_contexts[r], grad_resids[r]
        )
    input_grad = assemble([b[0] for b in backs])

    mid = reduce_groups(grad_mid_w.reshape(groups, -1, local)).reshape(3, -1, local)
    qkv = reduce_groups(jnp.stack([b[1].reshape(-1, local) for b in backs])).reshape(3, local, local)
    rows = jnp.concatenate(
        [
            jnp.swapaxes(grad_vecs, 1, 2),
            jnp.stack([b[2][:, :, 0] for b in backs]),
        ],
        axis=1,
    )
    count = rows.shape[1]
    mine = sum(to_group(rows[r], r) for r in span)
    shift = jnp.sum(cotangent, axis=1)
    small = lax.psum(jnp.concatenate([mine, shift[None]]), "dp")
    hidden = inner_b.shape[0] // local
    inner_rows = small[G_INNER_B : G_INNER_B + hidden].reshape(-1)
    return (
        layer_out,
        input_grad,
        qkv[0],
        qkv[1],
        qkv[2],
        small[count - 3],
        small[count - 1],
        mid[0],
        small[G_OUT_B],
        small[G_GAIN1],
        small[G_SHIFT1],
        mid[1],
        inner_rows,
        mid[2].T,
        small[G_OUTER_B],
        small[G_GAIN2],
        small[count],
    )


def solution(mesh):
    wide = P("tensor", "dp")
    rows = P("tensor", None)
    flat = P("tensor")
    columns = P(None, "tensor")
    return jax.shard_map(
        shards,
        mesh=mesh,
        in_specs=(
            wide,
            wide,
            rows,
            rows,
            rows,
            flat,
            flat,
            columns,
            flat,
            flat,
            flat,
            rows,
            flat,
            rows,
            flat,
            flat,
            flat,
        ),
        out_specs=(
            wide,
            wide,
            rows,
            rows,
            rows,
            flat,
            flat,
            columns,
            flat,
            flat,
            flat,
            rows,
            flat,
            rows,
            flat,
            flat,
            flat,
        ),
        check_vma=False,
    )
```
